1024 devices in a mesh: fsdp: 16 (over z_hi, x, core), chan: 64 (over y, z_lo).
Axes of the slice: x: 4, y: 8, z: 16 (z_hi: 2, z_lo: 8; z = z_hi * 8 + z_lo), core: 2. Of those that a mesh axis runs over, the one named last changes fastest.
Arguments:
- hidden: bfloat16 [2048, 4096], P('fsdp'), may hold values from -6 to 6
- conv_out: bfloat16 [2048, 8192], P('fsdp', 'chan'), may hold values from -6 to 6
- state_in: float32 [8192, 16], P('chan'), may hold values from -6 to 6
- gate_weight: bfloat16 [4096, 8192], P('fsdp', 'chan'), may hold values from -0.09375 to 0.09375
- xproj_weight: bfloat16 [8192, 288], P('chan'), may hold values from -0.0625 to 0.0625
- dt_weight: bfloat16 [256, 8192], P(None, 'chan'), may hold values from -0.375 to 0.375
- dt_bias: float32 [8192], P('chan'), may hold values from -7 to -1
- a_log: float32 [8192, 16], P('chan'), may hold values from -1.5 to 2.77
- skip_gain: float32 [8192], P('chan'), may hold values from 0.25 to 1
- out_weight: bfloat16 [4096, 8192], P('fsdp', 'chan'), may hold values from -0.0625 to 0.0625
Outputs:
- mixed: bfloat16 [2048, 4096], P(('fsdp', 'chan'))
The draws below stay inside these ranges and needn't reach their ends.
All inputs are finite; a program needn't handle non-finite values.
Results may differ from the reference program's by a relative error of at most 0.007.
Values may be sent and summed in bfloat16 or wider, within the bound.
No kernel may reach another device: no remote copies, remote signals or barrier semaphores. Data moves between devices by JAX's collectives and lax.ppermute only.
A program may use at most 32 MiB of HBM per device.

```python
import jax
import jax.numpy as jnp
from jax import lax

D = 4096
INNER = 8192
STATE = 16
RANK = 256
LENGTH = 2048
PROJ = 288


def levels(rng, extent, split, least, top_value):
    level = 1.0
    for dim, blocks in split:
        draws = jax.random.uniform(jax.random.fold_in(jax.random.fold_in(rng, 6), dim), (blocks,), jnp.float32, least / len(split), top_value / len(split))
        level = level * jnp.repeat(jnp.exp(draws), extent[dim] // blocks).reshape((-1,) + (1,) * (len(extent) - 1 - dim))
    return level


def centred(own_key, shape, scale, most, shards=(), kind=jnp.bfloat16):
    result = scale * jax.random.normal(own_key, shape, jnp.float32)
    if shards:
        result = result * levels(own_key, shape, shards, -0.22, 0.18)
    return jnp.clip(result, -most, most).astype(kind)


def setup_inputs(seed: int = 0) -> dict:
    arg_keys = jax.random.split(jax.random.key(seed), 11)
    hidden = centred(arg_keys[0], (LENGTH, D), 1.0, 6.0, ((0, 16),))
    conv_out = centred(arg_keys[1], (LENGTH, INNER), 1.0, 6.0, ((0, 16), (1, 64)))
    state_in = centred(arg_keys[2], (INNER, STATE), 1.0, 6.0, ((0, 64),), jnp.float32)
    gate_weight = centred(arg_keys[3], (D, INNER), D ** -0.5, 0.09375, ((0, 16), (1, 64)))
    xproj_weight = centred(arg_keys[4], (INNER, PROJ), INNER ** -0.5, 0.0625, ((0, 64),))
    dt_weight = centred(arg_keys[5], (RANK, INNER), RANK ** -0.5, 0.375, ((1, 64),))
    dt_bias = jnp.clip(-7.0 + 6.0 * jax.random.uniform(arg_keys[6], (INNER,), jnp.float32) ** levels(arg_keys[6], (INNER,), ((0, 64),), -0.2, 0.2), -7.0, -1.0)
    a_log = jnp.clip(-1.5 + 4.27 * jax.random.uniform(arg_keys[7], (INNER, STATE), jnp.float32) ** levels(arg_keys[7], (INNER, STATE), ((0, 64),), -0.2, 0.2), -1.5, 2.77)
    skip_gain = jnp.clip(0.25 + 0.75 * jax.random.uniform(arg_keys[8], (INNER,), jnp.float32) ** levels(arg_keys[8], (INNER,), ((0, 64),), -0.2, 0.2), 0.25, 1.0)
    out_weight = centred(arg_keys[9], (D, INNER), INNER ** -0.5, 0.0625, ((0, 16), (1, 64)))
    return {"hidden": hidden, "conv_out": conv_out, "state_in": state_in, "gate_weight": gate_weight, "xproj_weight": xproj_weight, "dt_weight": dt_weight, "dt_bias": dt_bias, "a_log": a_log, "skip_gain": skip_gain, "out_weight": out_weight}


def reference(hidden, conv_out, state_in, gate_weight, xproj_weight, dt_weight, dt_bias, a_log, skip_gain, out_weight):
    gate_pre = jnp.dot(hidden, gate_weight, preferred_element_type=jnp.float32)
    projected = jnp.dot(conv_out, xproj_weight, preferred_element_type=jnp.float32)
    step_low = projected[:, :RANK].astype(jnp.bfloat16)
    in_coef = projected[:, RANK:RANK + STATE]
    out_coef = projected[:, RANK + STATE:]
    step_size = jax.nn.softplus(jnp.dot(step_low, dt_weight, preferred_element_type=jnp.float32) + dt_bias)
    decay_rate = -jnp.exp(a_log)
    inputs = conv_out.astype(jnp.float32)

    def advance(carry_state, step_items):
        step_row, input_row, in_row, out_row = step_items
        carry_state = jnp.exp(step_row[:, None] * decay_rate) * carry_state + (step_row * input_row)[:, None] * in_row[None, :]
        return carry_state, jnp.sum(carry_state * out_row[None, :], axis=1)

    last_state, scanned = lax.scan(advance, state_in, (step_size, inputs, in_coef, out_coef))
    gated = ((scanned + skip_gain * inputs) * jax.nn.silu(gate_pre)).astype(jnp.bfloat16)
    mixed = lax.dot_general(gated, out_weight, (((1,), (1,)), ((), ())), preferred_element_type=jnp.float32)
    return mixed.astype(jnp.bfloat16)
```

```python
import jax
import jax.numpy as jnp
from jax import lax
from jax.experimental import pallas as pl
from jax.experimental.pallas import tpu as pltpu
from jax.sharding import Mesh
from jax.sharding import PartitionSpec as P

STATE = 16
RANK = 256
FSDP = ("zh", "x", "core")
CHAN = ("y", "z")
FSDP_CHAN = FSDP + CHAN
SPLIT = {16: (2, 4, 2), 64: (8, 8)}
PAYLOAD = 24
LOG2E = 1.4426950408889634
VMEM = pl.BlockSpec(memory_space=pltpu.VMEM)
SMEM = pl.BlockSpec(memory_space=pltpu.SMEM)


def exchange(array, axes):
    return lax.all_to_all(array, axes, 0, 0, tiled=True)


def near_core(array):
    return pltpu.with_memory_space_constraint(array, pltpu.VMEM)


def project_kernel(xproj, conv, out):
    pieces, piece, rows = out.shape
    share = lax.dot_general(
        xproj[...], conv[...], (((1,), (1,)), ((), ())), preferred_element_type=jnp.float32
    )
    share = jnp.concatenate([share, share[RANK:]], axis=0).astype(out.dtype)
    used = share.shape[0] // piece
    out[:used] = share.reshape(used, piece, rows)
    if used < pieces:
        out[used:] = jnp.zeros((pieces - used, piece, rows), out.dtype)


def add_kernel(at, shares, out):
    _, piece, _ = shares.shape
    total = jnp.sum(shares[...].astype(jnp.float32), axis=0)
    high = total.astype(jnp.bfloat16).astype(jnp.float32)
    row = at[0] * piece + lax.broadcasted_iota(jnp.int32, total.shape, 0)
    chosen = jnp.where(row >= RANK + 2 * STATE, total - high, high).astype(jnp.bfloat16)
    out[...] = jnp.broadcast_to(chosen[None], out.shape)


def coefficients(proj, first, count):
    low = first + 2 * STATE
    return proj[first : first + count].astype(jnp.float32) + proj[low : low + count].astype(
        jnp.float32
    )


def step_sizes(low, dt_weight, dt_bias):
    v = lax.dot_general(
        low, dt_weight, (((0,), (0,)), ((), ())), preferred_element_type=jnp.float32
    )
    v = v + dt_bias
    return jnp.maximum(v, 0.0) + jnp.log1p(jnp.exp(-jnp.abs(v)))


def local_kernel(proj, conv, dt_weight, dt_bias, a_log, step_out, pay_out):
    rows = conv.shape[0]
    step = step_sizes(proj[:RANK], dt_weight[...], dt_bias[...])
    step_out[...] = step
    rate = -jnp.exp(a_log[...]) * LOG2E
    driven = step * conv[...].astype(jnp.float32)
    coef = coefficients(proj, RANK, STATE)
    state = jnp.zeros((STATE, step.shape[1]), jnp.float32)
    for t in range(rows):
        state = jnp.exp2(step[t : t + 1] * rate) * state + driven[t : t + 1] * coef[:, t : t + 1]
    total = jnp.sum(step, axis=0, keepdims=True)
    high = total.astype(jnp.bfloat16).astype(jnp.float32)
    rest = jnp.zeros((PAYLOAD - STATE - 2, step.shape[1]), jnp.float32)
    payload = jnp.concatenate([state, high, total - high, rest], axis=0).astype(jnp.bfloat16)
    pay_out[...] = jnp.broadcast_to(payload[None], pay_out.shape)


def gate_kernel(here, hidden, kept, swapped, out):
    n_x, depth, _ = kept.shape
    block = depth // 4
    total = jnp.zeros(out.shape, jnp.float32)
    for other, weight in enumerate((kept, swapped)):
        for back in range(n_x):
            for turn in range(2):
                line = (here[0] + turn) % 2 * n_x + (here[1] + n_x - back) % n_x
                at = (line * 2 + (here[2] + other) % 2) * block
                total += jnp.dot(
                    hidden[:, pl.ds(pl.multiple_of(at, block), block)],
                    weight[back, turn * block : (turn + 1) * block],
                    preferred_element_type=jnp.float32,
                )
    out[...] = total


def scan_kernel(step_in, proj, conv, a_log, skip, out, through):
    rows = conv.shape[0]
    rate = -jnp.exp(a_log[...]) * LOG2E
    step = step_in[...]
    inputs = conv[...].astype(jnp.float32)
    driven = step * inputs
    direct = skip[...] * inputs
    coefs = coefficients(proj, RANK, 2 * STATE)
    state = jnp.zeros((STATE, step.shape[1]), jnp.float32)
    summed = jnp.zeros((1, step.shape[1]), jnp.float32)
    for t in range(rows):
        now = step[t : t + 1]
        summed = summed + now
        through[t : t + 1] = summed
        state = jnp.exp2(now * rate) * state + driven[t : t + 1] * coefs[:STATE, t : t + 1]
        value = jnp.sum(state * coefs[STATE:, t : t + 1], axis=0, keepdims=True)
        out[t : t + 1] = value + direct[t : t + 1]


def gated_kernel(pos, through, local, proj, a_log, state_in, gathered, gate_pre, out, carried):
    rows = local.shape[0]
    rate = -jnp.exp(a_log[...]) * LOG2E
    state = state_in[...]
    for source in range(gathered.shape[0]):
        payload = gathered[source].astype(jnp.float32)
        total = payload[STATE : STATE + 1] + payload[STATE + 1 : STATE + 2]
        moved = jnp.exp2(total * rate) * state + payload[:STATE]
        state = jnp.where(source < pos[0], moved, state)
    coefs = coefficients(proj, RANK + STATE, STATE)
    for t in range(rows):
        left = jnp.exp2(through[t : t + 1] * rate) * state
        carried[t : t + 1] = jnp.sum(left * coefs[:, t : t + 1], axis=0, keepdims=True)
    gate = gate_pre[...]
    value = (carried[...] + local[...]) * (gate / (1.0 + jnp.exp(-gate)))
    out[...] = jnp.broadcast_to(value.astype(jnp.bfloat16)[None], out.shape)


def mix_kernel(here, gated, kept, swapped, out, total, staged):
    n_x, depth, _ = kept.shape
    block = depth // 4
    tiles, rows, lanes = total.shape
    pieces, height, _ = out.shape
    own = rows // pieces
    per = block // lanes
    for other, weight in enumerate((kept, swapped)):
        part = jnp.zeros((rows, block), jnp.float32)
        for back in range(n_x):
            for turn in range(2):
                line = (here[0] + turn) % 2 * n_x + (here[1] + n_x - back) % n_x
                part += lax.dot_general(
                    gated[line],
                    weight[back, (2 + turn) * block : (3 + turn) * block],
                    (((1,), (1,)), ((), ())),
                    preferred_element_type=jnp.float32,
                )
        for k in range(per):
            total[(here[2] + other) % 2 * per + k] = part[:, k * lanes : (k + 1) * lanes]
    for row in range(own):
        for tile in range(tiles):
            staged[pl.ds(row * tiles + tile, pieces, stride=height), :] = total[
                tile, pl.ds(row, pieces, stride=own), :
            ]
    out[...] = staged[...].astype(jnp.bfloat16).reshape(out.shape)


def last_kernel(shares, out, rows):
    own, width = out.shape
    pieces, height, lanes = shares.shape
    tiles = height // own
    lines = width // (tiles * lanes)
    total = shares[...].astype(jnp.float32).reshape(lines, pieces // lines, height, lanes)
    total = jnp.sum(total, axis=1)
    for line in range(lines):
        for row in range(own):
            for tile in range(tiles):
                at = (line * tiles + tile) * lanes
                rows[row : row + 1, at : at + lanes] = total[
                    line, row * tiles + tile : row * tiles + tile + 1
                ]
    out[...] = rows[...].astype(jnp.bfloat16)


def shards_for(sizes):
    n_zh, n_x, n_core, n_y, n_z = sizes
    n_f, n_c = n_zh * n_x * n_core, n_y * n_z

    def turned(flip):
        pairs = []
        for zh in range(n_zh):
            for x in range(n_x):
                for core in range(n_core):
                    for y in range(n_y):
                        source = ((zh * n_x + x) * n_core + core) * n_y + y
                        to_zh, to_x = (y // n_x + flip) % n_zh, y % n_x
                        target = ((to_zh * n_x + to_x) * n_core + core) * n_y + zh * n_x + x
                        pairs.append((source, target))
        return pairs

    def shards(
        hidden, conv_out, state_in, gate_weight, xproj_weight, dt_weight, dt_bias, a_log, skip_gain, out_weight
    ):
        rows, channels = conv_out.shape
        own = rows // n_c
        here = jnp.stack([lax.axis_index(axis) for axis in FSDP]).astype(jnp.int32)
        own_piece = lax.axis_index(CHAN).astype(jnp.int32)[None]
        position = lax.axis_index(FSDP).astype(jnp.int32)[None]
        bf16, f32 = jnp.bfloat16, jnp.float32
        shape = jax.ShapeDtypeStruct

        gate_far = lax.ppermute(gate_weight, "zh", [(0, 1), (1, 0)])
        out_near = lax.ppermute(out_weight, FSDP + ("y",), turned(0))
        out_far = lax.ppermute(out_weight, FSDP + ("y",), turned(1))

        used = xproj_weight.shape[1] + 2 * STATE
        piece = -(-used // (8 * n_c)) * 8
        shares = pl.pallas_call(project_kernel, out_shape=shape((n_c, piece, rows), bf16))(
            xproj_weight.T, conv_out
        )
        shares = exchange(shares, CHAN)
        summed = pl.pallas_call(
            add_kernel, in_specs=[SMEM, VMEM], out_shape=shape(shares.shape, bf16)
        )(own_piece, near_core(shares))
        proj = exchange(summed, CHAN).reshape(n_c * piece, rows)

        mine = jnp.concatenate([gate_weight, gate_far, out_near, out_far], axis=0)
        kept = [mine]
        for back in range(1, n_x):
            kept.append(lax.ppermute(mine, "x", [(i, (i + back) % n_x) for i in range(n_x)]))
        kept = jnp.stack(kept)
        swapped = near_core(lax.ppermute(kept, "core", [(0, 1), (1, 0)]))
        kept = near_core(kept)

        proj, log_rate = near_core(proj), a_log.T
        step, payload = pl.pallas_call(
            local_kernel,
            out_shape=(shape((rows, channels), f32), shape((n_f, PAYLOAD, channels), bf16)),
        )(proj, conv_out, dt_weight, dt_bias[None], log_rate)
        gathered = near_core(exchange(payload, FSDP))
        local, through = pl.pallas_call(
            scan_kernel, out_shape=(shape((rows, channels), f32),) * 2
        )(step, proj, conv_out, log_rate, skip_gain[None])
        gate_pre = pl.pallas_call(
            gate_kernel, in_specs=[SMEM] + [VMEM] * 3, out_shape=shape((rows, channels), f32)
        )(here, hidden, kept, swapped)
        gated = pl.pallas_call(
            gated_kernel,
            in_specs=[SMEM] + [VMEM] * 7,
            out_shape=shape((n_y, rows, channels), bf16),
            scratch_shapes=[pltpu.VMEM((rows, channels), f32)],
        )(position, through, local, proj, log_rate, state_in.T, gathered, gate_pre)
        line = near_core(exchange(gated, "y"))

        width = hidden.shape[1] // n_y
        lanes = min(128, width // n_core)
        tiles = width // lanes
        sums = pl.pallas_call(
            mix_kernel,
            in_specs=[SMEM] + [VMEM] * 3,
            out_shape=shape((n_c, own * tiles, lanes), bf16),
            scratch_shapes=[
                pltpu.VMEM((tiles, rows, lanes), f32),
                pltpu.VMEM((rows * tiles, lanes), f32),
            ],
        )(here, line, kept, swapped)
        sums = near_core(exchange(sums, CHAN))
        return pl.pallas_call(
            last_kernel,
            out_shape=jax.ShapeDtypeStruct((own, n_y * width), bf16),
            scratch_shapes=[pltpu.VMEM((own, n_y * width), f32)],
        )(sums)

    return shards


def solution(mesh):
    sizes = SPLIT[mesh.shape["fsdp"]] + SPLIT[mesh.shape["chan"]]
    torus = Mesh(mesh.devices.reshape(sizes), FSDP_CHAN)
    return jax.shard_map(
        shards_for(sizes),
        mesh=torus,
        in_specs=(
            P(FSDP, None),
            P(FSDP, CHAN),
            P(CHAN, None),
            P(FSDP, CHAN),
            P(CHAN, None),
            P(None, CHAN),
            P(CHAN),
            P(CHAN, None),
            P(CHAN),
            P(FSDP, CHAN),
        ),
        out_specs=P(FSDP_CHAN, None),
        check_vma=False,
    )
```

```python
import jax
import jax.numpy as jnp
from jax import lax
from jax.experimental import pallas as pl
from jax.experimental.pallas import tpu as pltpu
from jax.sharding import Mesh
from jax.sharding import PartitionSpec as P

STATE = 16
RANK = 256
FSDP = ("zh", "x", "core")
CHAN = ("y", "z")
FSDP_CHAN = FSDP + CHAN
SPLIT = {16: (2, 4, 2), 64: (8, 8)}
PAYLOAD = 24
LOG2E = 1.4426950408889634
VMEM = pl.BlockSpec(memory_space=pltpu.VMEM)
SMEM = pl.BlockSpec(memory_space=pltpu.SMEM)


def exchange(array, axes):
    return lax.all_to_all(array, axes, 0, 0, tiled=True)


def near_core(array):
    return pltpu.with_memory_space_constraint(array, pltpu.VMEM)


def project_kernel(xproj, conv, out):
    pieces, piece, rows = out.shape
    share = lax.dot_general(
        xproj[...], conv[...], (((1,), (1,)), ((), ())), preferred_element_type=jnp.float32
    )
    share = jnp.concatenate([share, share[RANK:]], axis=0).astype(out.dtype)
    used = share.shape[0] // piece
    out[:used] = share.reshape(used, piece, rows)
    if used < pieces:
        out[used:] = jnp.zeros((pieces - used, piece, rows), out.dtype)


def add_kernel(at, shares, out):
    _, piece, _ = shares.shape
    total = jnp.sum(shares[...].astype(jnp.float32), axis=0)
    high = total.astype(jnp.bfloat16).astype(jnp.float32)
    row = at[0] * piece + lax.broadcasted_iota(jnp.int32, total.shape, 0)
    chosen = jnp.where(row >= RANK + 2 * STATE, total - high, high).astype(jnp.bfloat16)
    out[...] = jnp.broadcast_to(chosen[None], out.shape)


def coefficients(proj, first, count):
    low = first + 2 * STATE
    return proj[first : first + count].astype(jnp.float32) + proj[low : low + count].astype(
        jnp.float32
    )


def step_sizes(low, dt_weight, dt_bias):
    v = lax.dot_general(
        low, dt_weight, (((0,), (0,)), ((), ())), preferred_element_type=jnp.float32
    )
    v = v + dt_bias
    return jnp.maximum(v, 0.0) + jnp.log1p(jnp.exp(-jnp.abs(v)))


def local_kernel(proj, conv, dt_weight, dt_bias, a_log, step_out, pay_out):
    rows = conv.shape[0]
    step = step_sizes(proj[:RANK], dt_weight[...], dt_bias[...])
    step_out[...] = step
    rate = -jnp.exp(a_log[...]) * LOG2E
    driven = step * conv[...].astype(jnp.float32)
    coef = coefficients(proj, RANK, STATE)
    state = jnp.zeros((STATE, step.shape[1]), jnp.float32)
    for t in range(rows):
        state = jnp.exp2(step[t : t + 1] * rate) * state + driven[t : t + 1] * coef[:, t : t + 1]
    total = jnp.sum(step, axis=0, keepdims=True)
    rest = jnp.broadcast_to(total, (PAYLOAD - STATE, step.shape[1]))
    payload = jnp.concatenate([state, rest], axis=0)
    pay_out[...] = jnp.broadcast_to(payload[None], pay_out.shape)


def chain_kernel(pos, a_log, gathered, all_out, own_out):
    rate = -jnp.exp(a_log[...]) * LOG2E
    state = jnp.zeros(rate.shape, jnp.float32)
    total = jnp.zeros((1, rate.shape[1]), jnp.float32)
    rest = PAYLOAD - STATE
    for source in range(gathered.shape[0]):

        @pl.when(pos[0] == source)
        def _(state=state, total=total):
            own_out[:STATE] = state
            own_out[STATE:] = jnp.broadcast_to(total, (rest, total.shape[1]))

        step = gathered[source, STATE : STATE + 1]
        state = jnp.exp2(step * rate) * state + gathered[source, :STATE]
        total = total + step
    all_out[:STATE] = state
    all_out[STATE:] = jnp.broadcast_to(total, (rest, total.shape[1]))


def gate_kernel(here, hidden, kept, swapped, out):
    n_x, depth, _ = kept.shape
    block = depth // 4
    total = jnp.zeros(out.shape, jnp.float32)
    for other, weight in enumerate((kept, swapped)):
        for back in range(n_x):
            for turn in range(2):
                line = (here[0] + turn) % 2 * n_x + (here[1] + n_x - back) % n_x
                at = (line * 2 + (here[2] + other) % 2) * block
                total += jnp.dot(
                    hidden[:, pl.ds(pl.multiple_of(at, block), block)],
                    weight[back, 2 * turn * block : (2 * turn + 1) * block],
                    preferred_element_type=jnp.float32,
                )
    out[...] = total


def scan_kernel(step_in, proj, conv, a_log, skip, out, through):
    rows = conv.shape[0]
    rate = -jnp.exp(a_log[...]) * LOG2E
    step = step_in[...]
    inputs = conv[...].astype(jnp.float32)
    driven = step * inputs
    direct = skip[...] * inputs
    coefs = coefficients(proj, RANK, 2 * STATE)
    state = jnp.zeros((STATE, step.shape[1]), jnp.float32)
    summed = jnp.zeros((1, step.shape[1]), jnp.float32)
    for t in range(rows):
        now = step[t : t + 1]
        summed = summed + now
        through[t : t + 1] = summed
        state = jnp.exp2(now * rate) * state + driven[t : t + 1] * coefs[:STATE, t : t + 1]
        value = jnp.sum(state * coefs[STATE:, t : t + 1], axis=0, keepdims=True)
        out[t : t + 1] = value + direct[t : t + 1]


def gated_kernel(through, local, proj, a_log, state_in, half, before, gate_pre, out, carried):
    rows = local.shape[0]
    rate = -jnp.exp(a_log[...]) * LOG2E
    state = state_in[...]
    for part in (half, before):
        state = jnp.exp2(part[STATE : STATE + 1] * rate) * state + part[:STATE]
    coefs = coefficients(proj, RANK + STATE, STATE)
    for t in range(rows):
        left = jnp.exp2(through[t : t + 1] * rate) * state
        carried[t : t + 1] = jnp.sum(left * coefs[:, t : t + 1], axis=0, keepdims=True)
    gate = gate_pre[...]
    value = (carried[...] + local[...]) * (gate / (1.0 + jnp.exp(-gate)))
    out[...] = jnp.broadcast_to(value.astype(jnp.bfloat16)[None], out.shape)


def mix_kernel(here, gated, kept, swapped, out, total, staged):
    n_x, depth, _ = kept.shape
    block = depth // 4
    tiles, rows, lanes = total.shape
    pieces, height, _ = out.shape
    own = rows // pieces
    per = block // lanes
    for other, weight in enumerate((kept, swapped)):
        part = jnp.zeros((rows, block), jnp.float32)
        for back in range(n_x):
            for turn in range(2):
                line = (here[0] + turn) % 2 * n_x + (here[1] + n_x - back) % n_x
                part += lax.dot_general(
                    gated[line],
                    weight[back, (2 * turn + 1) * block : (2 * turn + 2) * block],
                    (((1,), (1,)), ((), ())),
                    preferred_element_type=jnp.float32,
                )
        for k in range(per):
            total[(here[2] + other) % 2 * per + k] = part[:, k * lanes : (k + 1) * lanes]
    for row in range(own):
        for tile in range(tiles):
            staged[pl.ds(row * tiles + tile, pieces, stride=height), :] = total[
                tile, pl.ds(row, pieces, stride=own), :
            ]
    out[...] = staged[...].astype(jnp.bfloat16).reshape(out.shape)


def last_kernel(shares, out, rows):
    own, width = out.shape
    pieces, height, lanes = shares.shape
    tiles = height // own
    lines = width // (tiles * lanes)
    total = shares[...].astype(jnp.float32).reshape(lines, pieces // lines, height, lanes)
    total = jnp.sum(total, axis=1)
    for line in range(lines):
        for row in range(own):
            for tile in range(tiles):
                at = (line * tiles + tile) * lanes
                rows[row : row + 1, at : at + lanes] = total[
                    line, row * tiles + tile : row * tiles + tile + 1
                ]
    out[...] = rows[...].astype(jnp.bfloat16)


def shards_for(sizes):
    n_zh, n_x, n_core, n_y, n_z = sizes
    n_c = n_y * n_z

    def turned():
        pairs = []
        for zh in range(n_zh):
            for x in range(n_x):
                for core in range(n_core):
                    for y in range(n_y):
                        source = ((zh * n_x + x) * n_core + core) * n_y + y
                        to_zh, to_x = y // n_x, y % n_x
                        target = ((to_zh * n_x + to_x) * n_core + core) * n_y + zh * n_x + x
                        pairs.append((source, target))
        return pairs

    def shards(
        hidden, conv_out, state_in, gate_weight, xproj_weight, dt_weight, dt_bias, a_log, skip_gain, out_weight
    ):
        rows, channels = conv_out.shape
        own = rows // n_c
        here = jnp.stack([lax.axis_index(axis) for axis in FSDP]).astype(jnp.int32)
        own_piece = lax.axis_index(CHAN).astype(jnp.int32)[None]
        position = lax.axis_index(("x", "core")).astype(jnp.int32)[None]
        bf16, f32 = jnp.bfloat16, jnp.float32
        shape, near = jax.ShapeDtypeStruct, pltpu.VMEM

        turned_weight = lax.ppermute(out_weight, FSDP + ("y",), turned())
        pair = jnp.concatenate([gate_weight, turned_weight], axis=0)
        far = lax.ppermute(pair, "zh", [(0, 1), (1, 0)])

        used = xproj_weight.shape[1] + 2 * STATE
        piece = -(-used // (8 * n_c)) * 8
        shares = pl.pallas_call(project_kernel, out_shape=near((n_c, piece, rows), bf16))(
            xproj_weight.T, conv_out
        )
        shares = exchange(shares, CHAN)
        summed = pl.pallas_call(
            add_kernel, in_specs=[SMEM, VMEM], out_shape=shape(shares.shape, bf16)
        )(own_piece, near_core(shares))
        proj = exchange(summed, CHAN).reshape(n_c * piece, rows)

        mine = jnp.concatenate([pair, far], axis=0)
        kept = [mine]
        for back in range(1, n_x):
            kept.append(lax.ppermute(mine, "x", [(i, (i + back) % n_x) for i in range(n_x)]))
        kept = jnp.stack(kept)
        swapped = near_core(lax.ppermute(kept, "core", [(0, 1), (1, 0)]))
        kept = near_core(kept)

        proj, log_rate = near_core(proj), a_log.T
        step, payload = pl.pallas_call(
            local_kernel,
            out_shape=(near((rows, channels), f32), near((n_x * n_core, PAYLOAD, channels), f32)),
        )(proj, conv_out, dt_weight, dt_bias[None], log_rate)
        gathered = near_core(exchange(payload, ("x", "core")))
        half, before = pl.pallas_call(
            chain_kernel,
            in_specs=[SMEM, VMEM, VMEM],
            out_shape=(near((PAYLOAD, channels), f32),) * 2,
        )(position, log_rate, gathered)
        half = near_core(lax.ppermute(half, "zh", [(0, 1)]))
        local, through = pl.pallas_call(
            scan_kernel, out_shape=(near((rows, channels), f32),) * 2
        )(near_core(step), proj, conv_out, log_rate, skip_gain[None])
        gate_pre = pl.pallas_call(
            gate_kernel, in_specs=[SMEM] + [VMEM] * 3, out_shape=near((rows, channels), f32)
        )(here, hidden, kept, swapped)
        gated = pl.pallas_call(
            gated_kernel,
            out_shape=near((n_y, rows, channels), bf16),
            scratch_shapes=[pltpu.VMEM((rows, channels), f32)],
        )(
            near_core(through),
            near_core(local),
            proj,
            log_rate,
            state_in.T,
            half,
            near_core(before),
            near_core(gate_pre),
        )
        line = near_core(exchange(gated, "y"))

        width = hidden.shape[1] // n_y
        lanes = min(128, width // n_core)
        tiles = width // lanes
        sums = pl.pallas_call(
            mix_kernel,
            in_specs=[SMEM] + [VMEM] * 3,
            out_shape=near((n_c, own * tiles, lanes), bf16),
            scratch_shapes=[
                pltpu.VMEM((tiles, rows, lanes), f32),
                pltpu.VMEM((rows * tiles, lanes), f32),
            ],
        )(here, line, kept, swapped)
        sums = near_core(exchange(sums, CHAN))
        return pl.pallas_call(
            last_kernel,
            out_shape=jax.ShapeDtypeStruct((own, n_y * width), bf16),
            scratch_shapes=[pltpu.VMEM((own, n_y * width), f32)],
        )(sums)

    return shards


def solution(mesh):
    sizes = SPLIT[mesh.shape["fsdp"]] + SPLIT[mesh.shape["chan"]]
    torus = Mesh(mesh.devices.reshape(sizes), FSDP_CHAN)
    return jax.shard_map(
        shards_for(sizes),
        mesh=torus,
        in_specs=(
            P(FSDP, None),
            P(FSDP, CHAN),
            P(CHAN, None),
            P(FSDP, CHAN),
            P(CHAN, None),
            P(None, CHAN),
            P(CHAN),
            P(CHAN, None),
            P(CHAN),
            P(FSDP, CHAN),
        ),
        out_specs=P(FSDP_CHAN, None),
        check_vma=False,
    )
```

```python
import jax
import jax.numpy as jnp
from jax import lax
from jax.experimental import pallas as pl
from jax.experimental.pallas import tpu as pltpu
from jax.sharding import Mesh
from jax.sharding import PartitionSpec as P

STATE = 16
RANK = 256
FSDP = ("zh", "x", "core")
CHAN = ("y", "z")
FSDP_CHAN = FSDP + CHAN
SPLIT = {16: (2, 4, 2), 64: (8, 8)}
PAYLOAD = 24
GRANT = 16 << 20
LOG2E = 1.4426950408889634
VMEM = pl.BlockSpec(memory_space=pltpu.VMEM)
SMEM = pl.BlockSpec(memory_space=pltpu.SMEM)


def run(kernel, **settings):
    if kernel in (gate_kernel, mix_kernel, chain_kernel, gated_kernel):
        settings["compiler_params"] = pltpu.CompilerParams(vmem_limit_bytes=GRANT)
    return pl.pallas_call(kernel, **settings)


def exchange(array, axes):
    return lax.all_to_all(array, axes, 0, 0, tiled=True)


def near_core(array):
    return pltpu.with_memory_space_constraint(array, pltpu.VMEM)


def project_kernel(xproj, conv, out):
    pieces, piece, rows = out.shape
    share = lax.dot_general(
        xproj[...], conv[...], (((1,), (1,)), ((), ())), preferred_element_type=jnp.float32
    )
    share = jnp.concatenate([share, share[RANK:]], axis=0).astype(out.dtype)
    used = share.shape[0] // piece
    out[:used] = share.reshape(used, piece, rows)
    if used < pieces:
        out[used:] = jnp.zeros((pieces - used, piece, rows), out.dtype)


def add_kernel(at, shares, out):
    _, piece, _ = shares.shape
    total = jnp.sum(shares[...].astype(jnp.float32), axis=0)
    high = total.astype(jnp.bfloat16).astype(jnp.float32)
    row = at[0] * piece + lax.broadcasted_iota(jnp.int32, total.shape, 0)
    chosen = jnp.where(row >= RANK + 2 * STATE, total - high, high).astype(jnp.bfloat16)
    out[...] = jnp.broadcast_to(chosen[None], out.shape)


def coefficients(proj, first, count):
    low = first + 2 * STATE
    return proj[first : first + count].astype(jnp.float32) + proj[low : low + count].astype(
        jnp.float32
    )


def step_sizes(low, dt_weight, dt_bias):
    v = lax.dot_general(
        low, dt_weight, (((0,), (0,)), ((), ())), preferred_element_type=jnp.float32
    )
    v = v + dt_bias
    return jnp.maximum(v, 0.0) + jnp.log1p(jnp.exp(-jnp.abs(v)))


def local_kernel(proj, conv, dt_weight, dt_bias, a_log, step_out, pay_out):
    rows = conv.shape[0]
    step = step_sizes(proj[:RANK], dt_weight[...], dt_bias[...])
    step_out[...] = step
    rate = -jnp.exp(a_log[...]) * LOG2E
    driven = step * conv[...].astype(jnp.float32)
    coef = coefficients(proj, RANK, STATE)
    state = jnp.zeros((STATE, step.shape[1]), jnp.float32)
    for t in range(rows):
        state = jnp.exp2(step[t : t + 1] * rate) * state + driven[t : t + 1] * coef[:, t : t + 1]
    total = jnp.sum(step, axis=0, keepdims=True)
    rest = jnp.broadcast_to(total, (PAYLOAD - STATE, step.shape[1]))
    payload = jnp.concatenate([state, rest], axis=0)
    pay_out[...] = jnp.broadcast_to(payload[None], pay_out.shape)


def chain_kernel(pos, a_log, gathered, all_out, own_out):
    rate = -jnp.exp(a_log[...]) * LOG2E
    state = jnp.zeros(rate.shape, jnp.float32)
    total = jnp.zeros((1, rate.shape[1]), jnp.float32)
    rest = PAYLOAD - STATE
    for source in range(gathered.shape[0]):

        @pl.when(pos[0] == source)
        def _(state=state, total=total):
            own_out[:STATE] = state
            own_out[STATE:] = jnp.broadcast_to(total, (rest, total.shape[1]))

        step = gathered[source, STATE : STATE + 1]
        state = jnp.exp2(step * rate) * state + gathered[source, :STATE]
        total = total + step
    all_out[:STATE] = state
    all_out[STATE:] = jnp.broadcast_to(total, (rest, total.shape[1]))


def gate_kernel(zh, x, core, hidden, kept, swapped, out):
    n_x, depth, _ = kept.shape
    block = depth // 4
    total = jnp.zeros(out.shape, jnp.float32)
    for other, weight in enumerate((kept, swapped)):
        for back in range(n_x):
            for turn in range(2):
                line = (zh[0] + turn) % 2 * n_x + (x[0] + n_x - back) % n_x
                at = (line * 2 + (core[0] + other) % 2) * block
                total += jnp.dot(
                    hidden[:, pl.ds(pl.multiple_of(at, block), block)],
                    weight[back, 2 * turn * block : (2 * turn + 1) * block],
                    preferred_element_type=jnp.float32,
                )
    out[...] = total


def scan_kernel(step_in, proj, conv, a_log, skip, out, through):
    rows = conv.shape[0]
    rate = -jnp.exp(a_log[...]) * LOG2E
    step = step_in[...]
    inputs = conv[...].astype(jnp.float32)
    driven = step * inputs
    direct = skip[...] * inputs
    coefs = coefficients(proj, RANK, 2 * STATE)
    state = jnp.zeros((STATE, step.shape[1]), jnp.float32)
    summed = jnp.zeros((1, step.shape[1]), jnp.float32)
    for t in range(rows):
        now = step[t : t + 1]
        summed = summed + now
        through[t : t + 1] = summed
        state = jnp.exp2(now * rate) * state + driven[t : t + 1] * coefs[:STATE, t : t + 1]
        value = jnp.sum(state * coefs[STATE:, t : t + 1], axis=0, keepdims=True)
        out[t : t + 1] = value + direct[t : t + 1]


def gated_kernel(through, local, proj, a_log, state_in, half, before, gate_pre, out, carried):
    rows = local.shape[0]
    rate = -jnp.exp(a_log[...]) * LOG2E
    state = state_in[...]
    for part in (half, before):
        state = jnp.exp2(part[STATE : STATE + 1] * rate) * state + part[:STATE]
    coefs = coefficients(proj, RANK + STATE, STATE)
    for t in range(rows):
        left = jnp.exp2(through[t : t + 1] * rate) * state
        carried[t : t + 1] = jnp.sum(left * coefs[:, t : t + 1], axis=0, keepdims=True)
    gate = gate_pre[...]
    value = (carried[...] + local[...]) * (gate / (1.0 + jnp.exp(-gate)))
    out[...] = jnp.broadcast_to(value.astype(jnp.bfloat16)[None], out.shape)


def mix_kernel(zh, x, core, gated, kept, swapped, out, total, staged):
    n_x, depth, _ = kept.shape
    block = depth // 4
    tiles, rows, lanes = total.shape
    pieces, height, _ = out.shape
    own = rows // pieces
    per = block // lanes
    for other, weight in enumerate((kept, swapped)):
        part = jnp.zeros((rows, block), jnp.float32)
        for back in range(n_x):
            for turn in range(2):
                line = (zh[0] + turn) % 2 * n_x + (x[0] + n_x - back) % n_x
                part += lax.dot_general(
                    gated[line],
                    weight[back, (2 * turn + 1) * block : (2 * turn + 2) * block],
                    (((1,), (1,)), ((), ())),
                    preferred_element_type=jnp.float32,
                )
        for k in range(per):
            total[(core[0] + other) % 2 * per + k] = part[:, k * lanes : (k + 1) * lanes]
    for row in range(own):
        for tile in range(tiles):
            staged[pl.ds(row * tiles + tile, pieces, stride=height), :] = total[
                tile, pl.ds(row, pieces, stride=own), :
            ]
    out[...] = staged[...].astype(jnp.bfloat16).reshape(out.shape)


def last_kernel(shares, out, rows):
    own, width = out.shape
    pieces, height, lanes = shares.shape
    tiles = height // own
    lines = width // (tiles * lanes)
    total = shares[...].astype(jnp.float32).reshape(lines, pieces // lines, height, lanes)
    total = jnp.sum(total, axis=1)
    for line in range(lines):
        for row in range(own):
            for tile in range(tiles):
                at = (line * tiles + tile) * lanes
                rows[row : row + 1, at : at + lanes] = total[
                    line, row * tiles + tile : row * tiles + tile + 1
                ]
    out[...] = rows[...].astype(jnp.bfloat16)


def shards_for(sizes):
    n_zh, n_x, n_core, n_y, n_z = sizes
    n_c = n_y * n_z

    def turned():
        pairs = []
        for zh in range(n_zh):
            for x in range(n_x):
                for core in range(n_core):
                    for y in range(n_y):
                        source = ((zh * n_x + x) * n_core + core) * n_y + y
                        to_zh, to_x = y // n_x, y % n_x
                        target = ((to_zh * n_x + to_x) * n_core + core) * n_y + zh * n_x + x
                        pairs.append((source, target))
        return pairs

    def shards(
        hidden, conv_out, state_in, gate_weight, xproj_weight, dt_weight, dt_bias, a_log, skip_gain, out_weight
    ):
        rows, channels = conv_out.shape
        own = rows // n_c
        here = [lax.axis_index(axis).astype(jnp.int32)[None] for axis in FSDP]
        own_piece = lax.axis_index(CHAN).astype(jnp.int32)[None]
        position = lax.axis_index(("x", "core")).astype(jnp.int32)[None]
        bf16, f32 = jnp.bfloat16, jnp.float32
        shape, near = jax.ShapeDtypeStruct, pltpu.VMEM

        turned_weight = lax.ppermute(out_weight, FSDP + ("y",), turned())
        halves = [(0, 1), (1, 0)]
        gate_far = lax.ppermute(gate_weight, "zh", halves)
        turned_far = lax.ppermute(turned_weight, "zh", halves)

        used = xproj_weight.shape[1] + 2 * STATE
        piece = -(-used // (8 * n_c)) * 8
        shares = run(project_kernel, out_shape=near((n_c, piece, rows), bf16))(
            xproj_weight.T, conv_out
        )
        shares = exchange(shares, CHAN)
        summed = run(
            add_kernel, in_specs=[SMEM, VMEM], out_shape=shape(shares.shape, bf16)
        )(own_piece, near_core(shares))
        proj = exchange(summed, CHAN).reshape(n_c * piece, rows)

        mine = jnp.concatenate([gate_weight, turned_weight, gate_far, turned_far], axis=0)
        kept = [mine]
        for back in range(1, n_x):
            kept.append(lax.ppermute(mine, "x", [(i, (i + back) % n_x) for i in range(n_x)]))
        kept = jnp.stack(kept)
        swapped = near_core(lax.ppermute(kept, "core", [(0, 1), (1, 0)]))
        kept = near_core(kept)

        proj, log_rate = near_core(proj), a_log.T
        conv_near = conv_out
        step, payload = run(
            local_kernel,
            out_shape=(near((rows, channels), f32), near((n_x * n_core, PAYLOAD, channels), f32)),
        )(proj, conv_near, dt_weight, dt_bias[None], log_rate)
        gathered = near_core(exchange(payload, ("x", "core")))
        half, before = run(
            chain_kernel,
            in_specs=[SMEM, VMEM, VMEM],
            out_shape=(near((PAYLOAD, channels), f32),) * 2,
        )(position, log_rate, gathered)
        half = near_core(lax.ppermute(half, "zh", [(0, 1)]))
        local, through = run(
            scan_kernel, out_shape=(near((rows, channels), f32),) * 2
        )(near_core(step), proj, conv_near, log_rate, skip_gain[None])
        gate_pre = run(
            gate_kernel, in_specs=[SMEM] * 3 + [VMEM] * 3, out_shape=near((rows, channels), f32)
        )(*here, hidden, kept, swapped)
        gated = run(
            gated_kernel,
            out_shape=near((n_y, rows, channels), bf16),
            scratch_shapes=[pltpu.VMEM((rows, channels), f32)],
        )(
            near_core(through),
            near_core(local),
            proj,
            log_rate,
            state_in.T,
            half,
            near_core(before),
            near_core(gate_pre),
        )
        line = near_core(exchange(gated, "y"))

        width = hidden.shape[1] // n_y
        lanes = min(128, width // n_core)
        tiles = width // lanes
        sums = run(
            mix_kernel,
            in_specs=[SMEM] * 3 + [VMEM] * 3,
            out_shape=near((n_c, own * tiles, lanes), bf16),
            scratch_shapes=[
                pltpu.VMEM((tiles, rows, lanes), f32),
                pltpu.VMEM((rows * tiles, lanes), f32),
            ],
        )(*here, line, kept, swapped)
        sums = near_core(exchange(sums, CHAN))
        return run(
            last_kernel,
            out_shape=jax.ShapeDtypeStruct((own, n_y * width), bf16),
            scratch_shapes=[pltpu.VMEM((own, n_y * width), f32)],
        )(sums)

    return shards


def solution(mesh):
    sizes = SPLIT[mesh.shape["fsdp"]] + SPLIT[mesh.shape["chan"]]
    torus = Mesh(mesh.devices.reshape(sizes), FSDP_CHAN)
    return jax.shard_map(
        shards_for(sizes),
        mesh=torus,
        in_specs=(
            P(FSDP, None),
            P(FSDP, CHAN),
            P(CHAN, None),
            P(FSDP, CHAN),
            P(CHAN, None),
            P(None, CHAN),
            P(CHAN),
            P(CHAN, None),
            P(CHAN),
            P(FSDP, CHAN),
        ),
        out_specs=P(FSDP_CHAN, None),
        check_vma=False,
    )
```

```python
import jax
import jax.numpy as jnp
from jax import lax
from jax.experimental import pallas as pl
from jax.experimental.pallas import tpu as pltpu
from jax.sharding import Mesh
from jax.sharding import PartitionSpec as P

STATE = 16
RANK = 256
FSDP = ("zh", "x", "core")
CHAN = ("y", "z")
FSDP_CHAN = FSDP + CHAN
SPLIT = {16: (2, 4, 2), 64: (8, 8)}
PAYLOAD = 24
GRANT = 16 << 20
LOG2E = 1.4426950408889634
VMEM = pl.BlockSpec(memory_space=pltpu.VMEM)
SMEM = pl.BlockSpec(memory_space=pltpu.SMEM)


def run(kernel, **settings):
    if kernel in (gate_kernel, mix_kernel, chain_kernel, gated_kernel):
        settings["compiler_params"] = pltpu.CompilerParams(vmem_limit_bytes=GRANT)
    return pl.pallas_call(kernel, **settings)


def exchange(array, axes):
    return lax.all_to_all(array, axes, 0, 0, tiled=True)


def near_core(array):
    return pltpu.with_memory_space_constraint(array, pltpu.VMEM)


def project_kernel(xproj, conv, out):
    pieces, piece, rows = out.shape
    share = lax.dot_general(
        xproj[...], conv[...], (((1,), (1,)), ((), ())), preferred_element_type=jnp.float32
    )
    share = jnp.concatenate([share, share[RANK:]], axis=0).astype(out.dtype)
    used = share.shape[0] // piece
    out[:used] = share.reshape(used, piece, rows)
    if used < pieces:
        out[used:] = jnp.zeros((pieces - used, piece, rows), out.dtype)


def add_kernel(at, shares, out):
    _, piece, _ = shares.shape
    total = jnp.sum(shares[...].astype(jnp.float32), axis=0)
    high = total.astype(jnp.bfloat16).astype(jnp.float32)
    row = at[0] * piece + lax.broadcasted_iota(jnp.int32, total.shape, 0)
    chosen = jnp.where(row >= RANK + 2 * STATE, total - high, high).astype(jnp.bfloat16)
    out[...] = jnp.broadcast_to(chosen[None], out.shape)


def coefficients(proj, first, count):
    low = first + 2 * STATE
    return proj[first : first + count].astype(jnp.float32) + proj[low : low + count].astype(
        jnp.float32
    )


def step_sizes(low, dt_weight, dt_bias):
    v = lax.dot_general(
        low, dt_weight, (((0,), (0,)), ((), ())), preferred_element_type=jnp.float32
    )
    v = v + dt_bias
    return jnp.maximum(v, 0.0) + jnp.log1p(jnp.exp(-jnp.abs(v)))


def local_kernel(proj, conv, dt_weight, dt_bias, a_log, step_out, pay_out):
    rows = conv.shape[0]
    step = step_sizes(proj[:RANK], dt_weight[...], dt_bias[...])
    step_out[...] = step
    rate = -jnp.exp(a_log[...]) * LOG2E
    driven = step * conv[...].astype(jnp.float32)
    coef = coefficients(proj, RANK, STATE)
    state = jnp.zeros((STATE, step.shape[1]), jnp.float32)
    for t in range(rows):
        state = jnp.exp2(step[t : t + 1] * rate) * state + driven[t : t + 1] * coef[:, t : t + 1]
    total = jnp.sum(step, axis=0, keepdims=True)
    rest = jnp.broadcast_to(total, (PAYLOAD - STATE, step.shape[1]))
    payload = jnp.concatenate([state, rest], axis=0)
    pay_out[...] = jnp.broadcast_to(payload[None], pay_out.shape)


def chain_kernel(pos, a_log, gathered, all_out, own_out):
    rate = -jnp.exp(a_log[...]) * LOG2E
    state = jnp.zeros(rate.shape, jnp.float32)
    total = jnp.zeros((1, rate.shape[1]), jnp.float32)
    rest = PAYLOAD - STATE
    for source in range(gathered.shape[0]):

        @pl.when(pos[0] == source)
        def _(state=state, total=total):
            own_out[:STATE] = state
            own_out[STATE:] = jnp.broadcast_to(total, (rest, total.shape[1]))

        step = gathered[source, STATE : STATE + 1]
        state = jnp.exp2(step * rate) * state + gathered[source, :STATE]
        total = total + step
    all_out[:STATE] = state
    all_out[STATE:] = jnp.broadcast_to(total, (rest, total.shape[1]))


def gate_kernel(zh, x, core, hidden, kept, swapped, out):
    n_x, depth, _ = kept.shape
    block = depth // 4
    total = jnp.zeros(out.shape, jnp.float32)
    for other, weight in enumerate((kept, swapped)):
        for back in range(n_x):
            for turn in range(2):
                line = (zh[0] + turn) % 2 * n_x + (x[0] + n_x - back) % n_x
                at = (line * 2 + (core[0] + other) % 2) * block
                total += jnp.dot(
                    hidden[:, pl.ds(pl.multiple_of(at, block), block)],
                    weight[back, 2 * turn * block : (2 * turn + 1) * block],
                    preferred_element_type=jnp.float32,
                )
    out[...] = total


def scan_kernel(step_in, proj, conv, a_log, skip, out, through):
    rows = conv.shape[0]
    rate = -jnp.exp(a_log[...]) * LOG2E
    step = step_in[...]
    inputs = conv[...].astype(jnp.float32)
    driven = step * inputs
    direct = skip[...] * inputs
    coefs = coefficients(proj, RANK, 2 * STATE)
    state = jnp.zeros((STATE, step.shape[1]), jnp.float32)
    summed = jnp.zeros((1, step.shape[1]), jnp.float32)
    for t in range(rows):
        now = step[t : t + 1]
        summed = summed + now
        through[t : t + 1] = summed
        state = jnp.exp2(now * rate) * state + driven[t : t + 1] * coefs[:STATE, t : t + 1]
        value = jnp.sum(state * coefs[STATE:, t : t + 1], axis=0, keepdims=True)
        out[t : t + 1] = value + direct[t : t + 1]


def gated_kernel(through, local, proj, a_log, state_in, half, before, gate_pre, out, carried):
    rows = local.shape[0]
    rate = -jnp.exp(a_log[...]) * LOG2E
    state = state_in[...]
    for part in (half, before):
        state = jnp.exp2(part[STATE : STATE + 1] * rate) * state + part[:STATE]
    coefs = coefficients(proj, RANK + STATE, STATE)
    for t in range(rows):
        left = jnp.exp2(through[t : t + 1] * rate) * state
        carried[t : t + 1] = jnp.sum(left * coefs[:, t : t + 1], axis=0, keepdims=True)
    gate = gate_pre[...]
    value = (carried[...] + local[...]) * (gate / (1.0 + jnp.exp(-gate)))
    out[...] = jnp.broadcast_to(value.astype(jnp.bfloat16)[None], out.shape)


def mix_kernel(zh, x, core, gated, kept, swapped, out, total, staged):
    n_x, depth, _ = kept.shape
    block = depth // 4
    tiles, rows, lanes = total.shape
    pieces, height, _ = out.shape
    own = rows // pieces
    per = block // lanes
    for other, weight in enumerate((kept, swapped)):
        part = jnp.zeros((rows, block), jnp.float32)
        for back in range(n_x):
            for turn in range(2):
                line = (zh[0] + turn) % 2 * n_x + (x[0] + n_x - back) % n_x
                part += lax.dot_general(
                    gated[line],
                    weight[back, (2 * turn + 1) * block : (2 * turn + 2) * block],
                    (((1,), (1,)), ((), ())),
                    preferred_element_type=jnp.float32,
                )
        for k in range(per):
            total[(core[0] + other) % 2 * per + k] = part[:, k * lanes : (k + 1) * lanes]
    for row in range(own):
        for tile in range(tiles):
            staged[pl.ds(row * tiles + tile, pieces, stride=height), :] = total[
                tile, pl.ds(row, pieces, stride=own), :
            ]
    out[...] = staged[...].astype(jnp.bfloat16).reshape(out.shape)


def last_kernel(shares, out, rows):
    own, width = out.shape
    pieces, height, lanes = shares.shape
    tiles = height // own
    lines = width // (tiles * lanes)
    total = shares[...].astype(jnp.float32).reshape(lines, pieces // lines, height, lanes)
    total = jnp.sum(total, axis=1)
    for line in range(lines):
        for row in range(own):
            for tile in range(tiles):
                at = (line * tiles + tile) * lanes
                rows[row : row + 1, at : at + lanes] = total[
                    line, row * tiles + tile : row * tiles + tile + 1
                ]
    out[...] = rows[...].astype(jnp.bfloat16)


def shards_for(sizes):
    n_zh, n_x, n_core, n_y, n_z = sizes
    n_c = n_y * n_z

    def turned():
        pairs = []
        for zh in range(n_zh):
            for x in range(n_x):
                for core in range(n_core):
                    for y in range(n_y):
                        source = ((zh * n_x + x) * n_core + core) * n_y + y
                        to_zh, to_x = y // n_x, y % n_x
                        target = ((to_zh * n_x + to_x) * n_core + core) * n_y + zh * n_x + x
                        pairs.append((source, target))
        return pairs

    def shards(
        hidden, conv_out, state_in, gate_weight, xproj_weight, dt_weight, dt_bias, a_log, skip_gain, out_weight
    ):
        rows, channels = conv_out.shape
        own = rows // n_c
        here = [lax.axis_index(axis).astype(jnp.int32)[None] for axis in FSDP]
        own_piece = lax.axis_index(CHAN).astype(jnp.int32)[None]
        position = lax.axis_index(("x", "core")).astype(jnp.int32)[None]
        bf16, f32 = jnp.bfloat16, jnp.float32
        shape, near = jax.ShapeDtypeStruct, pltpu.VMEM

        turned_weight = lax.ppermute(out_weight, FSDP + ("y",), turned())
        pair = jnp.concatenate([gate_weight, turned_weight], axis=0)
        far = lax.ppermute(pair, "zh", [(0, 1), (1, 0)])

        used = xproj_weight.shape[1] + 2 * STATE
        piece = -(-used // (8 * n_c)) * 8
        shares = run(project_kernel, out_shape=near((n_c, piece, rows), bf16))(
            xproj_weight.T, conv_out
        )
        shares = exchange(shares, CHAN)
        summed = run(
            add_kernel, in_specs=[SMEM, VMEM], out_shape=shape(shares.shape, bf16)
        )(own_piece, near_core(shares))
        proj = exchange(summed, CHAN).reshape(n_c * piece, rows)

        mine = jnp.concatenate([pair, far], axis=0)
        kept = [mine]
        for back in range(1, n_x):
            kept.append(lax.ppermute(mine, "x", [(i, (i + back) % n_x) for i in range(n_x)]))
        kept = jnp.stack(kept)
        swapped = near_core(lax.ppermute(kept, "core", [(0, 1), (1, 0)]))
        kept = near_core(kept)

        proj, log_rate = near_core(proj), a_log.T
        conv_near = conv_out
        step, payload = run(
            local_kernel,
            out_shape=(near((rows, channels), f32), near((n_x * n_core, PAYLOAD, channels), f32)),
        )(proj, conv_near, dt_weight, dt_bias[None], log_rate)
        gathered = near_core(exchange(payload, ("x", "core")))
        half, before = run(
            chain_kernel,
            in_specs=[SMEM, VMEM, VMEM],
            out_shape=(near((PAYLOAD, channels), f32),) * 2,
        )(position, log_rate, gathered)
        half = near_core(lax.ppermute(half, "zh", [(0, 1)]))
        local, through = run(
            scan_kernel, out_shape=(near((rows, channels), f32),) * 2
        )(near_core(step), proj, conv_near, log_rate, skip_gain[None])
        gate_pre = run(
            gate_kernel, in_specs=[SMEM] * 3 + [VMEM] * 3, out_shape=near((rows, channels), f32)
        )(*here, hidden, kept, swapped)
        gated = run(
            gated_kernel,
            out_shape=near((n_y, rows, channels), bf16),
            scratch_shapes=[pltpu.VMEM((rows, channels), f32)],
        )(
            near_core(through),
            near_core(local),
            proj,
            log_rate,
            state_in.T,
            half,
            near_core(before),
            near_core(gate_pre),
        )
        line = near_core(exchange(gated, "y"))

        width = hidden.shape[1] // n_y
        lanes = min(128, width // n_core)
        tiles = width // lanes
        sums = run(
            mix_kernel,
            in_specs=[SMEM] * 3 + [VMEM] * 3,
            out_shape=near((n_c, own * tiles, lanes), bf16),
            scratch_shapes=[
                pltpu.VMEM((tiles, rows, lanes), f32),
                pltpu.VMEM((rows * tiles, lanes), f32),
            ],
        )(*here, line, kept, swapped)
        sums = near_core(exchange(sums, CHAN))
        return run(
            last_kernel,
            out_shape=jax.ShapeDtypeStruct((own, n_y * width), bf16),
            scratch_shapes=[pltpu.VMEM((own, n_y * width), f32)],
        )(sums)

    return shards


def solution(mesh):
    sizes = SPLIT[mesh.shape["fsdp"]] + SPLIT[mesh.shape["chan"]]
    torus = Mesh(mesh.devices.reshape(sizes), FSDP_CHAN)
    return jax.shard_map(
        shards_for(sizes),
        mesh=torus,
        in_specs=(
            P(FSDP, None),
            P(FSDP, CHAN),
            P(CHAN, None),
            P(FSDP, CHAN),
            P(CHAN, None),
            P(None, CHAN),
            P(CHAN),
            P(CHAN, None),
            P(CHAN),
            P(FSDP, CHAN),
        ),
        out_specs=P(FSDP_CHAN, None),
        check_vma=False,
    )
```

```python
import jax
import jax.numpy as jnp
from jax import lax
from jax.experimental import pallas as pl
from jax.experimental.pallas import tpu as pltpu
from jax.sharding import Mesh
from jax.sharding import PartitionSpec as P

STATE = 16
RANK = 256
FSDP = ("zh", "x", "core")
CHAN = ("y", "z")
FSDP_CHAN = FSDP + CHAN
SPLIT = {16: (2, 4, 2), 64: (8, 8)}
PAYLOAD = 24
GRANT = 16 << 20
LOG2E = 1.4426950408889634
VMEM = pl.BlockSpec(memory_space=pltpu.VMEM)
SMEM = pl.BlockSpec(memory_space=pltpu.SMEM)


def run(kernel, **settings):
    if kernel in (gate_kernel, mix_kernel, chain_kernel, gated_kernel):
        settings["compiler_params"] = pltpu.CompilerParams(vmem_limit_bytes=GRANT)
    return pl.pallas_call(kernel, **settings)


def exchange(array, axes):
    return lax.all_to_all(array, axes, 0, 0, tiled=True)


def near_core(array):
    return pltpu.with_memory_space_constraint(array, pltpu.VMEM)


def project_kernel(xproj, conv, out):
    pieces, piece, rows = out.shape
    share = lax.dot_general(
        xproj[...], conv[...], (((1,), (1,)), ((), ())), preferred_element_type=jnp.float32
    )
    share = jnp.concatenate([share, share[RANK:]], axis=0).astype(out.dtype)
    used = share.shape[0] // piece
    out[:used] = share.reshape(used, piece, rows)
    if used < pieces:
        out[used:] = jnp.zeros((pieces - used, piece, rows), out.dtype)


def add_kernel(at, shares, out):
    _, piece, _ = shares.shape
    total = jnp.sum(shares[...].astype(jnp.float32), axis=0)
    high = total.astype(jnp.bfloat16).astype(jnp.float32)
    row = at[0] * piece + lax.broadcasted_iota(jnp.int32, total.shape, 0)
    chosen = jnp.where(row >= RANK + 2 * STATE, total - high, high).astype(jnp.bfloat16)
    out[...] = jnp.broadcast_to(chosen[None], out.shape)


def coefficients(proj, first, count):
    low = first + 2 * STATE
    return proj[first : first + count].astype(jnp.float32) + proj[low : low + count].astype(
        jnp.float32
    )


def step_sizes(low, dt_weight, dt_bias):
    v = lax.dot_general(
        low, dt_weight, (((0,), (0,)), ((), ())), preferred_element_type=jnp.float32
    )
    v = v + dt_bias
    return jnp.maximum(v, 0.0) + jnp.log1p(jnp.exp(-jnp.abs(v)))


def local_kernel(proj, conv, dt_weight, dt_bias, a_log, step_out, pay_out):
    rows = conv.shape[0]
    step = step_sizes(proj[:RANK], dt_weight[...], dt_bias[...])
    step_out[...] = step
    rate = -jnp.exp(a_log[...]) * LOG2E
    driven = step * conv[...].astype(jnp.float32)
    coef = coefficients(proj, RANK, STATE)
    state = jnp.zeros((STATE, step.shape[1]), jnp.float32)
    for t in range(rows):
        state = jnp.exp2(step[t : t + 1] * rate) * state + driven[t : t + 1] * coef[:, t : t + 1]
    total = jnp.sum(step, axis=0, keepdims=True)
    rest = jnp.broadcast_to(total, (PAYLOAD - STATE, step.shape[1]))
    payload = jnp.concatenate([state, rest], axis=0)
    pay_out[...] = jnp.broadcast_to(payload[None], pay_out.shape)


def chain_kernel(pos, a_log, gathered, all_out, own_out):
    rate = -jnp.exp(a_log[...]) * LOG2E
    state = jnp.zeros(rate.shape, jnp.float32)
    total = jnp.zeros((1, rate.shape[1]), jnp.float32)
    rest = PAYLOAD - STATE
    for source in range(gathered.shape[0]):

        @pl.when(pos[0] == source)
        def _(state=state, total=total):
            own_out[:STATE] = state
            own_out[STATE:] = jnp.broadcast_to(total, (rest, total.shape[1]))

        step = gathered[source, STATE : STATE + 1]
        state = jnp.exp2(step * rate) * state + gathered[source, :STATE]
        total = total + step
    all_out[:STATE] = state
    all_out[STATE:] = jnp.broadcast_to(total, (rest, total.shape[1]))


def gate_kernel(zh, x, core, far_hidden, kept, swapped, out, hidden, done):
    parts = done.shape[0]
    height = hidden.shape[0] // parts
    fetches = []
    for part in range(parts):
        rows = pl.ds(part * height, height)
        fetches.append(pltpu.make_async_copy(far_hidden.at[rows], hidden.at[rows], done.at[part]))
    for fetch in fetches:
        fetch.start()
    for fetch in fetches:
        fetch.wait()
    n_x, depth, _ = kept.shape
    block = depth // 4
    total = jnp.zeros(out.shape, jnp.float32)
    for other, weight in enumerate((kept, swapped)):
        for back in range(n_x):
            for turn in range(2):
                line = (zh[0] + turn) % 2 * n_x + (x[0] + n_x - back) % n_x
                at = (line * 2 + (core[0] + other) % 2) * block
                total += jnp.dot(
                    hidden[:, pl.ds(pl.multiple_of(at, block), block)],
                    weight[back, 2 * turn * block : (2 * turn + 1) * block],
                    preferred_element_type=jnp.float32,
                )
    out[...] = total


def scan_kernel(step_in, proj, conv, a_log, skip, out, through):
    rows = conv.shape[0]
    rate = -jnp.exp(a_log[...]) * LOG2E
    step = step_in[...]
    inputs = conv[...].astype(jnp.float32)
    driven = step * inputs
    direct = skip[...] * inputs
    coefs = coefficients(proj, RANK, 2 * STATE)
    state = jnp.zeros((STATE, step.shape[1]), jnp.float32)
    summed = jnp.zeros((1, step.shape[1]), jnp.float32)
    for t in range(rows):
        now = step[t : t + 1]
        summed = summed + now
        through[t : t + 1] = summed
        state = jnp.exp2(now * rate) * state + driven[t : t + 1] * coefs[:STATE, t : t + 1]
        value = jnp.sum(state * coefs[STATE:, t : t + 1], axis=0, keepdims=True)
        out[t : t + 1] = value + direct[t : t + 1]


def gated_kernel(through, local, proj, a_log, state_in, half, before, gate_pre, out, carried):
    rows = local.shape[0]
    rate = -jnp.exp(a_log[...]) * LOG2E
    state = state_in[...]
    for part in (half, before):
        state = jnp.exp2(part[STATE : STATE + 1] * rate) * state + part[:STATE]
    coefs = coefficients(proj, RANK + STATE, STATE)
    for t in range(rows):
        left = jnp.exp2(through[t : t + 1] * rate) * state
        carried[t : t + 1] = jnp.sum(left * coefs[:, t : t + 1], axis=0, keepdims=True)
    gate = gate_pre[...]
    value = (carried[...] + local[...]) * (gate / (1.0 + jnp.exp(-gate)))
    out[...] = jnp.broadcast_to(value.astype(jnp.bfloat16)[None], out.shape)


def mix_kernel(zh, x, core, gated, kept, swapped, out, total, staged):
    n_x, depth, _ = kept.shape
    block = depth // 4
    tiles, rows, lanes = total.shape
    pieces, height, _ = out.shape
    own = rows // pieces
    per = block // lanes
    for other, weight in enumerate((kept, swapped)):
        part = jnp.zeros((rows, block), jnp.float32)
        for back in range(n_x):
            for turn in range(2):
                line = (zh[0] + turn) % 2 * n_x + (x[0] + n_x - back) % n_x
                part += lax.dot_general(
                    gated[line],
                    weight[back, (2 * turn + 1) * block : (2 * turn + 2) * block],
                    (((1,), (1,)), ((), ())),
                    preferred_element_type=jnp.float32,
                )
        for k in range(per):
            total[(core[0] + other) % 2 * per + k] = part[:, k * lanes : (k + 1) * lanes]
    for row in range(own):
        for tile in range(tiles):
            staged[pl.ds(row * tiles + tile, pieces, stride=height), :] = total[
                tile, pl.ds(row, pieces, stride=own), :
            ]
    out[...] = staged[...].astype(jnp.bfloat16).reshape(out.shape)


def last_kernel(shares, out, rows):
    own, width = out.shape
    pieces, height, lanes = shares.shape
    tiles = height // own
    lines = width // (tiles * lanes)
    total = shares[...].astype(jnp.float32).reshape(lines, pieces // lines, height, lanes)
    total = jnp.sum(total, axis=1)
    for line in range(lines):
        for row in range(own):
            for tile in range(tiles):
                at = (line * tiles + tile) * lanes
                rows[row : row + 1, at : at + lanes] = total[
                    line, row * tiles + tile : row * tiles + tile + 1
                ]
    out[...] = rows[...].astype(jnp.bfloat16)


def shards_for(sizes):
    n_zh, n_x, n_core, n_y, n_z = sizes
    n_c = n_y * n_z

    def turned():
        pairs = []
        for zh in range(n_zh):
            for x in range(n_x):
                for core in range(n_core):
                    for y in range(n_y):
                        source = ((zh * n_x + x) * n_core + core) * n_y + y
                        to_zh, to_x = y // n_x, y % n_x
                        target = ((to_zh * n_x + to_x) * n_core + core) * n_y + zh * n_x + x
                        pairs.append((source, target))
        return pairs

    def shards(
        hidden, conv_out, state_in, gate_weight, xproj_weight, dt_weight, dt_bias, a_log, skip_gain, out_weight
    ):
        rows, channels = conv_out.shape
        own = rows // n_c
        here = [lax.axis_index(axis).astype(jnp.int32)[None] for axis in FSDP]
        own_piece = lax.axis_index(CHAN).astype(jnp.int32)[None]
        position = lax.axis_index(("x", "core")).astype(jnp.int32)[None]
        bf16, f32 = jnp.bfloat16, jnp.float32
        shape, near = jax.ShapeDtypeStruct, pltpu.VMEM

        turned_weight = lax.ppermute(out_weight, FSDP + ("y",), turned())
        pair = jnp.concatenate([gate_weight, turned_weight], axis=0)
        far = lax.ppermute(pair, "zh", [(0, 1), (1, 0)])

        used = xproj_weight.shape[1] + 2 * STATE
        piece = -(-used // (8 * n_c)) * 8
        shares = run(project_kernel, out_shape=near((n_c, piece, rows), bf16))(
            xproj_weight.T, conv_out
        )
        shares = exchange(shares, CHAN)
        summed = run(
            add_kernel, in_specs=[SMEM, VMEM], out_shape=shape(shares.shape, bf16)
        )(own_piece, near_core(shares))
        proj = exchange(summed, CHAN).reshape(n_c * piece, rows)

        mine = jnp.concatenate([pair, far], axis=0)
        kept = [mine]
        for back in range(1, n_x):
            kept.append(lax.ppermute(mine, "x", [(i, (i + back) % n_x) for i in range(n_x)]))
        kept = jnp.stack(kept)
        swapped = near_core(lax.ppermute(kept, "core", [(0, 1), (1, 0)]))
        kept = near_core(kept)

        proj, log_rate = near_core(proj), a_log.T
        conv_near = conv_out
        step, payload = run(
            local_kernel,
            out_shape=(near((rows, channels), f32), near((n_x * n_core, PAYLOAD, channels), f32)),
        )(proj, conv_near, dt_weight, dt_bias[None], log_rate)
        gathered = near_core(exchange(payload, ("x", "core")))
        half, before = run(
            chain_kernel,
            in_specs=[SMEM, VMEM, VMEM],
            out_shape=(near((PAYLOAD, channels), f32),) * 2,
        )(position, log_rate, gathered)
        half = near_core(lax.ppermute(half, "zh", [(0, 1)]))
        local, through = run(
            scan_kernel, out_shape=(near((rows, channels), f32),) * 2
        )(near_core(step), proj, conv_near, log_rate, skip_gain[None])
        gate_pre = run(
            gate_kernel,
            in_specs=[SMEM] * 3 + [pl.BlockSpec(memory_space=pltpu.HBM)] + [VMEM] * 2,
            out_shape=near((rows, channels), f32),
            scratch_shapes=[pltpu.VMEM(hidden.shape, bf16), pltpu.SemaphoreType.DMA((4,))],
        )(*here, pltpu.with_memory_space_constraint(hidden, pltpu.HBM), kept, swapped)
        gated = run(
            gated_kernel,
            out_shape=near((n_y, rows, channels), bf16),
            scratch_shapes=[pltpu.VMEM((rows, channels), f32)],
        )(
            near_core(through),
            near_core(local),
            proj,
            log_rate,
            state_in.T,
            half,
            near_core(before),
            near_core(gate_pre),
        )
        line = near_core(exchange(gated, "y"))

        width = hidden.shape[1] // n_y
        lanes = min(128, width // n_core)
        tiles = width // lanes
        sums = run(
            mix_kernel,
            in_specs=[SMEM] * 3 + [VMEM] * 3,
            out_shape=near((n_c, own * tiles, lanes), bf16),
            scratch_shapes=[
                pltpu.VMEM((tiles, rows, lanes), f32),
                pltpu.VMEM((rows * tiles, lanes), f32),
            ],
        )(*here, line, kept, swapped)
        sums = near_core(exchange(sums, CHAN))
        return run(
            last_kernel,
            out_shape=jax.ShapeDtypeStruct((own, n_y * width), bf16),
            scratch_shapes=[pltpu.VMEM((own, n_y * width), f32)],
        )(sums)

    return shards


def solution(mesh):
    sizes = SPLIT[mesh.shape["fsdp"]] + SPLIT[mesh.shape["chan"]]
    torus = Mesh(mesh.devices.reshape(sizes), FSDP_CHAN)
    return jax.shard_map(
        shards_for(sizes),
        mesh=torus,
        in_specs=(
            P(FSDP, None),
            P(FSDP, CHAN),
            P(CHAN, None),
            P(FSDP, CHAN),
            P(CHAN, None),
            P(None, CHAN),
            P(CHAN),
            P(CHAN, None),
            P(CHAN),
            P(FSDP, CHAN),
        ),
        out_specs=P(FSDP_CHAN, None),
        check_vma=False,
    )
```
